32 devices in a mesh: section: 4 (over y, x), tile: 8 (over z, core).
Axes of the slice: x: 2, y: 2, z: 4, core: 2. Of those that a mesh axis runs over, the one named last changes fastest.
Arguments:
- stored_inputs: bfloat16 [4, 4, 24, 128, 1024], P('section', None, 'tile'), may hold values from -6 to 6
- cotangent: bfloat16 [4, 24, 128, 1024], P(None, 'tile'), may hold values from -6 to 6
- w_reduce: bfloat16 [4, 1024, 256], P('section'), may hold values from -0.1875 to 0.1875
- w_spatial: bfloat16 [4, 2304, 256], P('section'), may hold values from -0.125 to 0.125
- w_expand: bfloat16 [4, 256, 1024], P('section'), may hold values from -0.375 to 0.375
- bias_reduce: float32 [4, 256], P('section'), may hold values from -1 to 1
- bias_spatial: float32 [4, 256], P('section'), may hold values from -1 to 1
- bias_expand: float32 [4, 1024], P('section'), may hold values from 0.5 to 2
Outputs:
- input_grads: bfloat16 [4, 4, 24, 128, 1024], P('section', None, 'tile')
- grad_reduce: float32 [4, 1024, 256], P('section', 'tile')
- grad_spatial: float32 [4, 2304, 256], P('section', 'tile')
- grad_expand: float32 [4, 256, 1024], P('section', 'tile')
The draws below stay inside these ranges and needn't reach their ends.
All inputs are finite; a program needn't handle non-finite values.
Results may differ from the reference program's by a relative error of at most 0.024.
Values may be sent and summed in bfloat16 or wider, within the bound.
A program may use at most 64 MiB of HBM per device.

```python
import jax
import jax.numpy as jnp
from jax import lax

D = 1024
B = 256
COLS = 128
MICRO = 4
SECTIONS = 4
HEIGHT = 24


def block_scale(stream_key, shape, cuts, low, high):
    def one(position, blocks):
        draws = jax.random.uniform(jax.random.fold_in(jax.random.fold_in(stream_key, 6), position), (blocks,), jnp.float32, low / len(cuts), high / len(cuts))
        return jnp.repeat(jnp.exp(draws), shape[position] // blocks).reshape((-1,) + (1,) * (len(shape) - position - 1))

    gain = one(*cuts[0])
    for cut in cuts[1:]:
        gain = gain * one(*cut)
    return gain


def normal_values(key, extent, scale, bound, shards=(), dtype=jnp.bfloat16):
    gain = block_scale(key, extent, shards, -0.22, 0.18) if shards else 1.0
    array = jax.random.normal(key, extent, jnp.float32) * scale * gain
    return jnp.minimum(jnp.maximum(array, -bound), bound).astype(dtype)


def setup_inputs(seed: int = 0) -> dict:
    seeds = jax.random.split(jax.random.key(seed), 9)
    return {
        "stored_inputs": normal_values(seeds[0], (SECTIONS, MICRO, HEIGHT, COLS, D), 1.0, 6.0, ((0, 4), (2, 8))),
        "cotangent": normal_values(seeds[1], (MICRO, HEIGHT, COLS, D), 1.0, 6.0, ((1, 8),)),
        "w_reduce": normal_values(seeds[2], (SECTIONS, D, B), D ** -0.5, 0.1875, ((0, 4),)),
        "w_spatial": normal_values(seeds[3], (SECTIONS, 9 * B, B), (9 * B) ** -0.5, 0.125, ((0, 4),)),
        "w_expand": normal_values(seeds[4], (SECTIONS, B, D), B ** -0.5, 0.375, ((0, 4),)),
        "bias_reduce": jnp.clip(jax.random.uniform(seeds[5], (SECTIONS, B), jnp.float32, -1.0, 1.0) * block_scale(seeds[5], (SECTIONS, B), ((0, 4),), -0.4, 0.0), -1.0, 1.0),
        "bias_spatial": jnp.clip(jax.random.uniform(seeds[6], (SECTIONS, B), jnp.float32, -1.0, 1.0) * block_scale(seeds[6], (SECTIONS, B), ((0, 4),), -0.4, 0.0), -1.0, 1.0),
        "bias_expand": jnp.clip(0.5 + 1.5 * jax.random.uniform(seeds[7], (SECTIONS, D), jnp.float32) ** block_scale(seeds[7], (SECTIONS, D), ((0, 4),), -0.2, 0.2), 0.5, 2.0),
    }


def silu_slope(pre_act):
    sigma_val = jax.nn.sigmoid(pre_act)
    return sigma_val * (1.0 + pre_act * (1.0 - sigma_val))


def tap_views(padded, flip_sign):
    row_count = padded.shape[-3] - 2
    col_count = padded.shape[-2]
    widened = jnp.pad(padded, [(0, 0)] * (padded.ndim - 2) + [(1, 1), (0, 0)])
    pieces_list = []
    for row_off in (-1, 0, 1):
        for col_off in (-1, 0, 1):
            row_start = 1 + flip_sign * row_off
            col_start = 1 + flip_sign * col_off
            window = lax.slice_in_dim(widened, row_start, row_start + row_count, axis=widened.ndim - 3)
            window = lax.slice_in_dim(window, col_start, col_start + col_count, axis=widened.ndim - 2)
            pieces_list.append(window)
    return jnp.concatenate(pieces_list, axis=-1)


def contract_rows(left_mat, right_mat):
    return lax.dot_general(left_mat, right_mat, (((0,), (0,)), ((), ())), preferred_element_type=jnp.float32)


def contract_cols(left_mat, right_mat):
    return lax.dot_general(left_mat, right_mat, (((1,), (1,)), ((), ())), preferred_element_type=jnp.float32)


def reference(stored_inputs, cotangent, w_reduce, w_spatial, w_expand, bias_reduce, bias_spatial, bias_expand):
    section_count, micro_count, height, width_px, model_w = stored_inputs.shape
    bottle = w_reduce.shape[2]
    pixels = height * width_px
    sums_one = [jnp.zeros((model_w, bottle), jnp.float32) for section_id in range(section_count)]
    sums_two = [jnp.zeros((9 * bottle, bottle), jnp.float32) for section_id in range(section_count)]
    sums_three = [jnp.zeros((bottle, model_w), jnp.float32) for section_id in range(section_count)]
    results = [[None] * micro_count for section_id in range(section_count)]
    for micro_id in range(micro_count):
        upstream = cotangent[micro_id]
        for section_id in range(section_count - 1, -1, -1):
            flat_in = stored_inputs[section_id, micro_id].reshape(pixels, model_w)
            pre_one = jnp.dot(flat_in, w_reduce[section_id], preferred_element_type=jnp.float32) + bias_reduce[section_id]
            act_one = jax.nn.silu(pre_one).astype(jnp.bfloat16)
            padded = jnp.pad(act_one.reshape(height, width_px, bottle), ((1, 1), (0, 0), (0, 0)))
            patches = tap_views(padded, 1).reshape(pixels, 9 * bottle)
            pre_two = jnp.dot(patches, w_spatial[section_id], preferred_element_type=jnp.float32) + bias_spatial[section_id]
            act_two = jax.nn.silu(pre_two).astype(jnp.bfloat16)
            pre_three = jnp.dot(act_two, w_expand[section_id], preferred_element_type=jnp.float32) + bias_expand[section_id] + flat_in.astype(jnp.float32)
            slope_three = upstream.reshape(pixels, model_w).astype(jnp.float32) * silu_slope(pre_three)
            grad_three = slope_three.astype(jnp.bfloat16)
            sums_three[section_id] = sums_three[section_id] + contract_rows(act_two, grad_three)
            grad_two = (contract_cols(grad_three, w_expand[section_id]) * silu_slope(pre_two)).astype(jnp.bfloat16)
            sums_two[section_id] = sums_two[section_id] + contract_rows(patches, grad_two)
            grad_pad = jnp.pad(grad_two.reshape(height, width_px, bottle), ((1, 1), (0, 0), (0, 0)))
            back_patches = tap_views(grad_pad, -1).reshape(pixels, 9 * bottle)
            w_turned = w_spatial[section_id].reshape(9, bottle, bottle).transpose(0, 2, 1).reshape(9 * bottle, bottle)
            spatial_back = jnp.dot(back_patches, w_turned, preferred_element_type=jnp.float32)
            grad_one = (spatial_back * silu_slope(pre_one)).astype(jnp.bfloat16)
            sums_one[section_id] = sums_one[section_id] + contract_rows(flat_in, grad_one)
            input_grad = (contract_cols(grad_one, w_reduce[section_id]) + slope_three).astype(jnp.bfloat16)
            upstream = input_grad.reshape(height, width_px, model_w)
            results[section_id][micro_id] = upstream
    input_grads = jnp.stack([jnp.stack(results[section_id]) for section_id in range(section_count)])
    return input_grads, jnp.stack(sums_one), jnp.stack(sums_two), jnp.stack(sums_three)
```

```python
import functools

import jax
import jax.numpy as jnp
from jax import lax
from jax.experimental import pallas as pl
from jax.experimental.pallas import tpu as pltpu
from jax.sharding import PartitionSpec as P

BF = jnp.bfloat16
F32 = jnp.float32
PAD = 8
WIDTH = 16
TAPER = 8


def silu_and_slope(pre_act):
    sigma_val = jax.nn.sigmoid(pre_act)
    return pre_act * sigma_val, sigma_val * (1.0 + pre_act * (1.0 - sigma_val))


def dot_nn(left, right):
    return jnp.dot(left, right, preferred_element_type=F32)


def dot_tn(left, right):
    return lax.dot_general(left, right, (((0,), (0,)), ((), ())), preferred_element_type=F32)


def kernel(
    sections, tiles, x_in, cot_ref, w1_in, w2_in, w3_in, b1_ref, b2_ref, b3_ref,
    gin_out, o1_ref, o2_ref, o3_ref,
    x_ref, w1_ref, w2_ref, w3_ref, gin_ref,
    up, slope1, slope2, slope3, act_pad, taps, act2, g_pad, g3, g2, g1,
    t1, t2, t3, fe_out, fe_in, be_out, be_in, sum1, sum2, sum3,
    p1, p2, p3, q1, q2, q3, r1, r2, r3, u1, u2, u3, d1, d2, d3,
    x_sem, w_sem, gin_sem, cot_sem, up_ss, up_rs, fe_ss, fe_rs, be_ss, be_rs, a_ss, a_rs, z_ss, zu_rs, zd_rs,
):
    micros, rows, cols, model = x_ref.shape
    bottle = w1_ref.shape[1]
    pixels = rows * cols
    cuts = cut_columns(cols)
    pieces = len(cuts)
    half = tiles // 2
    sec = lax.axis_index("section")
    tile = lax.axis_index("tile")
    core = lax.rem(tile, 2)
    zed = tile // 2
    is_last = sec == sections - 1
    has_above = tile > 0
    has_below = tile < tiles - 1
    chip_above = zed > 0
    chip_below = zed < half - 1
    partner = tile + 1 - 2 * core

    def x_copy(m):
        return pltpu.make_async_copy(x_in.at[m], x_ref.at[m], x_sem.at[m])

    def w_copy(n):
        src, dst = ((w1_in, w1_ref), (w2_in, w2_ref), (w3_in, w3_ref))[n]
        return pltpu.make_async_copy(src, dst, w_sem.at[n])

    def cot_copy(m):
        return pltpu.make_async_copy(cot_ref.at[m], up.at[m], cot_sem.at[m])

    def gin_copy(m):
        return pltpu.make_async_copy(gin_ref.at[m], gin_out.at[m], gin_sem.at[m])

    w_copy(0).start()
    x_copy(0).start()
    w_copy(1).start()
    w_copy(2).start()
    for m in range(1, micros):
        x_copy(m).start()

    barrier = pltpu.get_barrier_semaphore()

    def greet(cond, target):
        @pl.when(cond)
        def _():
            pl.semaphore_signal(barrier, inc=1, device_id=target, device_id_type=pl.DeviceIdType.MESH)

    greet(has_above, {"tile": tile - 1})
    greet(has_below, {"tile": tile + 1})
    greet(chip_above, {"tile": tile - 2})
    greet(chip_below, {"tile": tile + 2})
    greet(sec > 0, {"section": sec - 1})
    greet(sec < sections - 1, {"section": sec + 1})

    @pl.when(is_last)
    def _():
        for m in range(micros):
            cot_copy(m).start()

    def clear_rim(pad):
        tall, wide = pad.shape[1], pad.shape[2]
        for m in range(micros):
            for y in (0, tall - 1):
                pad[m, y] = jnp.zeros((wide, bottle), F32)
            for y in range(1, tall - 1):
                for c in (0, wide - PAD):
                    pad[m, y, pl.ds(c, PAD)] = jnp.zeros((PAD, bottle), F32)

    clear_rim(act_pad)

    def remote(src, dst, ss, rs, target):
        return pltpu.make_async_remote_copy(
            src_ref=src, dst_ref=dst, send_sem=ss, recv_sem=rs,
            device_id=target, device_id_type=pl.DeviceIdType.MESH,
        )

    def fe_up(m):
        return remote(fe_out.at[m, 0], fe_in.at[m, 1], fe_ss.at[m, 0], fe_rs.at[m, 1], {"tile": tile - 1})

    def fe_down(m):
        return remote(fe_out.at[m, 1], fe_in.at[m, 0], fe_ss.at[m, 1], fe_rs.at[m, 0], {"tile": tile + 1})

    def cut(j):
        return pl.ds(*cuts[j])

    def be_up(m, j):
        n = m * pieces + j
        return remote(
            be_out.at[m, 0, cut(j)], be_in.at[m, 1, cut(j)], be_ss.at[n, 0], be_rs.at[n, 1],
            {"tile": tile - 1},
        )

    def be_down(m, j):
        n = m * pieces + j
        return remote(
            be_out.at[m, 1, cut(j)], be_in.at[m, 0, cut(j)], be_ss.at[n, 1], be_rs.at[n, 0],
            {"tile": tile + 1},
        )

    def relay(m, j):
        n = m * pieces + j
        return remote(
            gin_ref.at[m, :, cut(j)], up.at[m, :, cut(j)], up_ss.at[n], up_rs.at[n],
            {"section": sec - 1},
        )

    def reduce_in(m, _):
        x_copy(m).wait()
        for y in range(rows):
            pre = dot_nn(x_ref[m, y], w1_ref[...]) + b1_ref[...]
            act, slope = silu_and_slope(pre)
            slope1[m, y] = slope
            act = act.astype(BF)
            act_pad[m, y + 1, pl.ds(PAD, cols)] = act.astype(F32)
            if y == 0:
                fe_out[m, 0] = act
            if y == rows - 1:
                fe_out[m, 1] = act
        return 0

    w_copy(0).wait()
    reduce_in(0, 0)

    greetings = (
        has_above.astype(jnp.int32) + has_below.astype(jnp.int32) + chip_above.astype(jnp.int32)
        + chip_below.astype(jnp.int32) + (sec > 0).astype(jnp.int32) + (sec < sections - 1).astype(jnp.int32)
    )
    pl.semaphore_wait(barrier, greetings)

    def share_rims(m):
        @pl.when(has_above)
        def _():
            fe_up(m).start()

        @pl.when(has_below)
        def _():
            fe_down(m).start()

    def reduce_and_share(m, _):
        reduce_in(m, 0)
        share_rims(m)
        return 0

    share_rims(0)
    w_copy(1).wait()
    w_copy(2).wait()
    for n in range(model // bottle):
        lanes = pl.ds(n * bottle, bottle)
        t1[:, lanes] = w1_ref[lanes, :].astype(F32).T.astype(BF)
        t3[lanes, :] = w3_ref[:, lanes].astype(F32).T.astype(BF)
    for n in range(9):
        band = pl.ds(n * bottle, bottle)
        t2[band, :] = w2_ref[band, :].astype(F32).T.astype(BF)
    clear_rim(g_pad)
    sum1[...] = jnp.zeros(sum1.shape, F32)
    sum2[...] = jnp.zeros(sum2.shape, F32)
    sum3[...] = jnp.zeros(sum3.shape, F32)

    def expand_out(m, _):
        @pl.when(has_above)
        def _():
            fe_down(m).wait_recv()
            act_pad[m, 0, pl.ds(PAD, cols)] = fe_in[m, 0].astype(F32)

        @pl.when(has_below)
        def _():
            fe_up(m).wait_recv()
            act_pad[m, rows + 1, pl.ds(PAD, cols)] = fe_in[m, 1].astype(F32)

        for shift in range(3):
            for y in range(rows + 2):
                taps[shift, m, y] = act_pad[m, y, pl.ds(PAD - 1 + shift, cols)].astype(BF)
        for y in range(rows):
            patch = jnp.concatenate(
                [taps[dx, m, y + dy] for dy in range(3) for dx in range(3)], axis=-1
            )
            pre = dot_nn(patch, w2_ref[...]) + b2_ref[...]
            act, slope = silu_and_slope(pre)
            slope2[m, y] = slope
            act = act.astype(BF)
            act2[m, y] = act
            for n in range(model // bottle):
                lanes = pl.ds(n * bottle, bottle)
                pre = dot_nn(act, w3_ref[:, lanes]) + b3_ref[:, lanes] + x_ref[m, y, :, lanes].astype(F32)
                slope3[m, y, :, lanes] = silu_and_slope(pre)[1]
        return 0

    def outer_part(m, first, last):
        turn = lax.rem(m, 2)
        begin = cuts[first][0]
        width = sum(cuts[last]) - begin
        span = pl.ds(begin, width)
        for y in range(rows):
            g3[turn, y, span] = (up[m, y, span].astype(F32) * slope3[m, y, span]).astype(BF)
        back = dot_nn(g3[turn, :, span].reshape(rows * width, model), t3[...])
        grad = (back.reshape(rows, width, bottle) * slope2[m, :, span]).astype(BF)
        g2[turn, :, span] = grad
        g_pad[m, pl.ds(1, rows), pl.ds(PAD + begin, width)] = grad.astype(F32)
        be_out[m, 0, span] = grad[0]
        be_out[m, 1, span] = grad[rows - 1]

        @pl.when(has_above)
        def _():
            for j in range(first, last + 1):
                be_up(m, j).start()

        @pl.when(has_below)
        def _():
            for j in range(first, last + 1):
                be_down(m, j).start()

    def take_rims(m, j):
        @pl.when(has_above)
        def _():
            be_down(m, j).wait_recv()
            g_pad[m, 0, pl.ds(PAD + cuts[j][0], cuts[j][1])] = be_in[m, 0, cut(j)].astype(F32)

        @pl.when(has_below)
        def _():
            be_up(m, j).wait_recv()
            g_pad[m, rows + 1, pl.ds(PAD + cuts[j][0], cuts[j][1])] = be_in[m, 1, cut(j)].astype(F32)

    def inner_part(m, first, last):
        turn = lax.rem(m, 2)
        begin = cuts[first][0]
        width = sum(cuts[last]) - begin
        span = pl.ds(begin, width)
        moved = [
            g_pad[m, :, pl.ds(PAD + 1 + begin - dx, width)].astype(BF) for dx in range(3)
        ]
        patch = jnp.concatenate(
            [
                moved[dx][2 - dy : 2 - dy + rows].reshape(rows * width, bottle)
                for dy in range(3)
                for dx in range(3)
            ],
            axis=-1,
        )
        total = dot_nn(patch, t2[...])
        grad = (total.reshape(rows, width, bottle) * slope1[m, :, span]).astype(BF)
        g1[turn, :, span] = grad
        flat = grad.reshape(rows * width, bottle)
        for n in range(model // bottle):
            lanes = pl.ds(n * bottle, bottle)
            back = dot_nn(flat, t1[:, lanes]).reshape(rows, width, bottle)
            direct = up[m, :, span, lanes].astype(F32) * slope3[m, :, span, lanes]
            gin_ref[m, :, span, lanes] = (back + direct).astype(BF)

        @pl.when(sec > 0)
        def _():
            for j in range(first, last + 1):
                relay(m, j).start()

        if last == pieces - 1:
            gin_copy(m).start()

    def add_three(m, n):
        lanes = pl.ds(n * bottle, bottle)
        turn = lax.rem(m, 2)
        sum3[:, lanes] += dot_tn(
            act2[m].reshape(pixels, bottle), g3[turn, :, :, lanes].reshape(pixels, bottle)
        )

    def add_two(m, n):
        turn = lax.rem(m, 2)
        patch = taps[n % 3, m, pl.ds(n // 3, rows)].reshape(pixels, bottle)
        sum2[pl.ds(n * bottle, bottle)] += dot_tn(patch, g2[turn].reshape(pixels, bottle))

    def add_one(m, n):
        lanes = pl.ds(n * bottle, bottle)
        turn = lax.rem(m, 2)
        sum1[lanes] += dot_tn(
            x_ref[m, :, :, lanes].reshape(pixels, bottle), g1[turn].reshape(pixels, bottle)
        )

    count = model // bottle
    threes = [functools.partial(add_three, n=n) for n in range(count)]
    twos = [functools.partial(add_two, n=n) for n in range(9)]
    ones = [functools.partial(add_one, n=n) for n in range(count)]
    adds = threes + twos + ones
    final = micros - 1

    @pl.when(is_last)
    def _():
        def stream(m, _):
            expand_out(m, 0)
            cot_copy(m).wait()
            early = min(2, pieces - 1)
            outer_part(m, 0, early)
            if early < pieces - 1:
                outer_part(m, early + 1, pieces - 1)
            taken = 0
            for first in range(0, pieces - 1, 2):
                last = first + 1 if first + 3 < pieces else pieces - 1
                if first > 0 and last < first:
                    continue
                until = min(last + 2, pieces)
                for j in range(taken, until):
                    take_rims(m, j)
                taken = until
                inner_part(m, first, last)
                if last == pieces - 1:
                    break

            @pl.when(m == 0)
            def _():
                lax.fori_loop(1, micros, reduce_and_share, 0)

            @pl.when(m < final)
            def _():
                for add in adds:
                    add(m)

            return 0

        lax.fori_loop(0, micros, stream, 0)

    @pl.when(jnp.logical_not(is_last))
    def _():
        lax.fori_loop(1, micros, reduce_and_share, 0)
        lax.fori_loop(0, micros, expand_out, 0)

        def stream(m, _):
            left = list(adds)
            for j in range(pieces):
                relay(m, j).wait_recv()
                outer_part(m, j, j)
                if j == 0:
                    @pl.when(m > 0)
                    def _():
                        take_rims(m - 1, pieces - 1)
                        inner_part(m - 1, pieces - 2, pieces - 1)

                    continue

                take_rims(m, j - 1)
                if 0 <= j - 2 < pieces - 2:
                    inner_part(m, j - 2, j - 2)
                share = -(-len(left) // (pieces - j))

                @pl.when(m > 0)
                def _():
                    for add in left[:share]:
                        add(m - 1)

                left = left[share:]
            return 0

        lax.fori_loop(0, micros, stream, 0)

    kinds = (
        (sum3, p3, q3, r3, u3, d3, o3_ref),
        (sum2, p2, q2, r2, u2, d2, o2_ref),
        (sum1, p1, q1, r1, u1, d1, o1_ref),
    )

    def swap(kind):
        return remote(kinds[kind][1], kinds[kind][2], a_ss.at[kind], a_rs.at[kind], {"tile": partner})

    def hop_down(kind, d):
        n = kind * half + d
        return remote(
            kinds[kind][3].at[d], kinds[kind][4].at[d], z_ss.at[n], zd_rs.at[n], {"tile": tile + 2}
        )

    def hop_up(kind, d):
        n = kind * half + d
        return remote(
            kinds[kind][3].at[d], kinds[kind][5].at[d], z_ss.at[n], zu_rs.at[n], {"tile": tile - 2}
        )

    def start_swap(kind):
        total, sent, out = kinds[kind][0], kinds[kind][1], kinds[kind][6]
        span = out.shape[0]
        for z in range(half):
            first = pl.multiple_of((2 * z + 1 - core) * span, 16)
            sent[z] = total[pl.ds(first, span)].astype(BF)
        swap(kind).start()

    def make_part(kind):
        total, _, got, part, _, _, out = kinds[kind]
        span = out.shape[0]
        swap(kind).wait_recv()
        for z in range(half):
            first = pl.multiple_of((2 * z + core) * span, 16)
            part[z] = (total[pl.ds(first, span)] + got[z].astype(F32)).astype(BF)
        own = pl.multiple_of((2 * zed + core) * span, 16)
        out[...] = total[pl.ds(own, span)] + got[zed].astype(F32)

    def send_ends(kind, step):
        @pl.when(jnp.logical_not(chip_above))
        def _():
            hop_down(kind, half - 1 - step).start()

        @pl.when(jnp.logical_not(chip_below))
        def _():
            hop_up(kind, step).start()

    def carry_down(kind, step):
        part, down = kinds[kind][3], kinds[kind][4]
        d = half - 1 - step

        @pl.when(jnp.logical_and(chip_above, zed < d))
        def _():
            hop_down(kind, d).wait_recv()
            part[d] = (part[d].astype(F32) + down[d].astype(F32)).astype(BF)
            hop_down(kind, d).start()

    def carry_up(kind, step):
        part, over = kinds[kind][3], kinds[kind][5]

        @pl.when(jnp.logical_and(chip_below, zed > step))
        def _():
            hop_up(kind, step).wait_recv()
            part[step] = (part[step].astype(F32) + over[step].astype(F32)).astype(BF)
            hop_up(kind, step).start()

    def end_chain(kind):
        _, _, _, _, down, over, out = kinds[kind]

        @pl.when(chip_above)
        def _():
            hop_down(kind, zed).wait_recv()
            out[...] += down[zed].astype(F32)

        @pl.when(chip_below)
        def _():
            hop_up(kind, zed).wait_recv()
            out[...] += over[zed].astype(F32)

    for add in twos:
        add(final)
    start_swap(1)
    for add in threes:
        add(final)
    start_swap(0)
    make_part(1)
    send_ends(1, 0)

    @pl.when(jnp.logical_not(is_last))
    def _():
        take_rims(final, pieces - 1)
        inner_part(final, pieces - 2, pieces - 1)

    for add in ones:
        add(final)
    start_swap(2)
    make_part(0)
    send_ends(0, 0)
    make_part(2)
    send_ends(2, 0)
    order = (1, 0, 2)
    for step in range(1, half - 1):
        for kind in order:
            send_ends(kind, step)
    upper = zed < half // 2
    for near, carries in ((upper, (carry_down, carry_up)), (jnp.logical_not(upper), (carry_up, carry_down))):
        @pl.when(near)
        def _():
            for step in range(half - 1):
                for carry in carries:
                    for kind in order:
                        carry(kind, step)


    def close(m, _):
        gin_copy(m).wait()

        @pl.when(has_above)
        def _():
            fe_up(m).wait_send()
            for j in range(pieces):
                be_up(m, j).wait_send()

        @pl.when(has_below)
        def _():
            fe_down(m).wait_send()
            for j in range(pieces):
                be_down(m, j).wait_send()

        @pl.when(sec > 0)
        def _():
            for j in range(pieces):
                relay(m, j).wait_send()

        return 0

    lax.fori_loop(0, micros, close, 0)
    for kind in range(3):
        end_chain(kind)
    for kind in range(3):
        swap(kind).wait_send()
        for d in range(half):
            @pl.when(zed < d)
            def _():
                hop_down(kind, d).wait_send()

            @pl.when(zed > d)
            def _():
                hop_up(kind, d).wait_send()


def cut_columns(cols):
    wide = (cols - 2 * TAPER) // WIDTH
    cuts = [(n * WIDTH, WIDTH) for n in range(wide)]
    return cuts + [(n, TAPER) for n in range(wide * WIDTH, cols, TAPER)]


def hand_over(*refs):
    count = len(refs) // 4
    ins, outs, holds, sems = (refs[n * count : (n + 1) * count] for n in range(4))
    arrive, leave = [], []
    for a, o, h, s in zip(ins, outs, holds, sems):
        for n in range(h.shape[0] if len(h.shape) > 2 else 1):
            pick = (lambda r: r.at[n]) if len(h.shape) > 2 else (lambda r: r)
            arrive.append(pltpu.make_async_copy(pick(a), pick(h), s.at[0, n]))
            leave.append(pltpu.make_async_copy(pick(h), pick(o), s.at[1, n]))
    for copy in arrive:
        copy.start()
    for one, two in zip(arrive, leave):
        one.wait()
        two.start()
    for copy in leave:
        copy.wait()


def local(
    sections, tiles,
    stored_inputs, cotangent, w_reduce, w_spatial, w_expand, bias_reduce, bias_spatial, bias_expand,
):
    _, micros, rows, cols, model = stored_inputs.shape
    bottle = w_reduce.shape[2]
    half = tiles // 2
    spans = (model // tiles, 9 * bottle // tiles, bottle // tiles)
    wides = (bottle, bottle, model)
    vmem = pltpu.VMEM
    dma = pltpu.SemaphoreType.DMA
    whole = pl.BlockSpec(memory_space=pltpu.VMEM)
    there = pl.BlockSpec(memory_space=pl.ANY)
    scratch = [
        vmem((micros, rows, cols, model), BF),
        vmem((model, bottle), BF),
        vmem((9 * bottle, bottle), BF),
        vmem((bottle, model), BF),
        vmem((micros, rows, cols, model), BF),
        vmem((micros, rows, cols, model), BF),
        vmem((micros, rows, cols, bottle), F32),
        vmem((micros, rows, cols, bottle), F32),
        vmem((micros, rows, cols, model), F32),
        vmem((micros, rows + 2, cols + 2 * PAD, bottle), F32),
        vmem((3, micros, rows + 2, cols, bottle), BF),
        vmem((micros, rows, cols, bottle), BF),
        vmem((micros, rows + 2, cols + 2 * PAD, bottle), F32),
        vmem((2, rows, cols, model), BF),
        vmem((2, rows, cols, bottle), BF),
        vmem((2, rows, cols, bottle), BF),
    ]
    scratch += [vmem((bottle, model), BF), vmem((9 * bottle, bottle), BF), vmem((model, bottle), BF)]
    scratch += [vmem((micros, 2, cols, bottle), BF)] * 4
    scratch += [vmem((span * tiles, wide), F32) for span, wide in zip(spans, wides)]
    for _ in range(5):
        scratch += [vmem((half, span, wide), BF) for span, wide in zip(spans, wides)]
    pieces = micros * len(cut_columns(cols))
    scratch += [
        dma((micros,)), dma((3,)), dma((micros,)),
        dma((micros,)), dma((pieces,)), dma((pieces,)), dma((micros, 2)), dma((micros, 2)),
        dma((pieces, 2)), dma((pieces, 2)), dma((3,)), dma((3,)), dma((3 * half,)), dma((3 * half,)), dma((3 * half,)),
    ]
    shapes = [jax.ShapeDtypeStruct((micros, rows, cols, model), BF)] + [
        jax.ShapeDtypeStruct((span, wide), F32) for span, wide in zip(spans, wides)
    ]
    outs = pl.pallas_call(
        functools.partial(kernel, sections, tiles),
        out_shape=shapes,
        in_specs=[there] * 5 + [whole] * 3,
        out_specs=[there] + [whole] * 3,
        scratch_shapes=scratch,
        compiler_params=pltpu.CompilerParams(
            collective_id=0, has_side_effects=True, vmem_limit_bytes=66 * 1024 * 1000
        ),
    )(
        stored_inputs[0], cotangent, w_reduce[0], w_spatial[0], w_expand[0],
        bias_reduce, bias_spatial, bias_expand,
    )
    outs = pl.pallas_call(
        hand_over,
        out_shape=shapes,
        in_specs=[there] * 4,
        out_specs=[there] * 4,
        scratch_shapes=[vmem(shape.shape, shape.dtype) for shape in shapes] + [dma((2, micros))] * 4,
    )(*outs)
    return tuple(out[None] for out in outs)


def solution(mesh):
    return jax.shard_map(
        functools.partial(local, mesh.shape["section"], mesh.shape["tile"]),
        mesh=mesh,
        in_specs=(
            P("section", None, "tile", None, None),
            P(None, "tile", None, None),
            P("section", None, None),
            P("section", None, None),
            P("section", None, None),
            P("section", None),
            P("section", None),
            P("section", None),
        ),
        out_specs=(
            P("section", None, "tile", None, None),
            P("section", "tile", None),
            P("section", "tile", None),
            P("section", "tile", None),
        ),
        check_vma=False,
    )
```

```python
import functools

import jax
import jax.numpy as jnp
from jax import lax
from jax.experimental import pallas as pl
from jax.experimental.pallas import tpu as pltpu
from jax.sharding import PartitionSpec as P

BF = jnp.bfloat16
F32 = jnp.float32
PAD = 8
WIDTH = 8
LAG = 3
GROUP = 4


def silu_and_slope(pre_act):
    sigma_val = jax.nn.sigmoid(pre_act)
    return pre_act * sigma_val, sigma_val * (1.0 + pre_act * (1.0 - sigma_val))


def dot_nn(left, right):
    return jnp.dot(left, right, preferred_element_type=F32)


def dot_tn(left, right):
    return lax.dot_general(left, right, (((0,), (0,)), ((), ())), preferred_element_type=F32)


def kernel(
    sections, tiles, x_in, cot_ref, w1_in, w2_in, w3_in, b1_ref, b2_ref, b3_ref,
    gin_out, o1_ref, o2_ref, o3_ref,
    x_ref, w1_ref, w2_ref, w3_ref, gin_ref,
    up, slope1, slope2, slope3, act_pad, taps, act2, g_pad, g3, g2, g1,
    t1, t2, t3, fe_out, fe_in, be_out, be_in, sum1, sum2, sum3,
    p1, p2, p3, q1, q2, q3, r1, r2, r3, u1, u2, u3, d1, d2, d3,
    x_sem, w_sem, gin_sem, cot_sem, up_ss, up_rs, fe_ss, fe_rs, be_ss, be_rs, a_ss, a_rs, z_ss, zu_rs, zd_rs,
):
    micros, rows, cols, model = x_ref.shape
    bottle = w1_ref.shape[1]
    pixels = rows * cols
    cuts = cut_columns(cols)
    pieces = len(cuts)
    half = tiles // 2
    sec = lax.axis_index("section")
    tile = lax.axis_index("tile")
    core = lax.rem(tile, 2)
    zed = tile // 2
    is_last = sec == sections - 1
    has_above = tile > 0
    has_below = tile < tiles - 1
    chip_above = zed > 0
    chip_below = zed < half - 1
    partner = tile + 1 - 2 * core

    def x_copy(m):
        return pltpu.make_async_copy(x_in.at[m], x_ref.at[m], x_sem.at[m])

    def w_copy(n):
        src, dst = ((w1_in, w1_ref), (w2_in, w2_ref), (w3_in, w3_ref))[n]
        return pltpu.make_async_copy(src, dst, w_sem.at[n])

    def cot_copy(m):
        return pltpu.make_async_copy(cot_ref.at[m], up.at[m], cot_sem.at[m])

    def gin_copy(m):
        return pltpu.make_async_copy(gin_ref.at[m], gin_out.at[m], gin_sem.at[m])

    w_copy(0).start()
    x_copy(0).start()
    w_copy(1).start()
    w_copy(2).start()
    for m in range(1, micros):
        x_copy(m).start()

    barrier = pltpu.get_barrier_semaphore()

    def greet(cond, target):
        @pl.when(cond)
        def _():
            pl.semaphore_signal(barrier, inc=1, device_id=target, device_id_type=pl.DeviceIdType.MESH)

    greet(has_above, {"tile": tile - 1})
    greet(has_below, {"tile": tile + 1})
    greet(chip_above, {"tile": tile - 2})
    greet(chip_below, {"tile": tile + 2})
    greet(sec > 0, {"section": sec - 1})
    greet(sec < sections - 1, {"section": sec + 1})

    @pl.when(is_last)
    def _():
        for m in range(micros):
            cot_copy(m).start()

    def clear_rim(pad):
        tall, wide = pad.shape[1], pad.shape[2]
        for m in range(micros):
            for y in (0, tall - 1):
                pad[m, y] = jnp.zeros((wide, bottle), F32)
            for y in range(1, tall - 1):
                for c in (0, wide - PAD):
                    pad[m, y, pl.ds(c, PAD)] = jnp.zeros((PAD, bottle), F32)

    clear_rim(act_pad)

    def remote(src, dst, ss, rs, target):
        return pltpu.make_async_remote_copy(
            src_ref=src, dst_ref=dst, send_sem=ss, recv_sem=rs,
            device_id=target, device_id_type=pl.DeviceIdType.MESH,
        )

    def fe_up(m):
        return remote(fe_out.at[m, 0], fe_in.at[m, 1], fe_ss.at[m, 0], fe_rs.at[m, 1], {"tile": tile - 1})

    def fe_down(m):
        return remote(fe_out.at[m, 1], fe_in.at[m, 0], fe_ss.at[m, 1], fe_rs.at[m, 0], {"tile": tile + 1})

    def cut(j):
        return pl.ds(*cuts[j])

    def be_up(m, j):
        n = m * pieces + j
        return remote(
            be_out.at[m, 0, cut(j)], be_in.at[m, 1, cut(j)], be_ss.at[n, 0], be_rs.at[n, 1],
            {"tile": tile - 1},
        )

    def be_down(m, j):
        n = m * pieces + j
        return remote(
            be_out.at[m, 1, cut(j)], be_in.at[m, 0, cut(j)], be_ss.at[n, 1], be_rs.at[n, 0],
            {"tile": tile + 1},
        )

    def relay(m, j):
        n = m * pieces + j
        return remote(
            gin_ref.at[m, :, cut(j)], up.at[m, :, cut(j)], up_ss.at[n], up_rs.at[n],
            {"section": sec - 1},
        )

    def reduce_in(m, _):
        x_copy(m).wait()
        pre = dot_nn(x_ref[m].reshape(pixels, model), w1_ref[...]) + b1_ref[...]
        act, slope = silu_and_slope(pre)
        slope1[m] = slope.reshape(rows, cols, bottle)
        act = act.astype(BF).reshape(rows, cols, bottle)
        act_pad[m, pl.ds(1, rows), pl.ds(PAD, cols)] = act.astype(F32)
        fe_out[m, 0] = act[0]
        fe_out[m, 1] = act[rows - 1]
        return 0

    w_copy(0).wait()
    reduce_in(0, 0)

    greetings = (
        has_above.astype(jnp.int32) + has_below.astype(jnp.int32) + chip_above.astype(jnp.int32)
        + chip_below.astype(jnp.int32) + (sec > 0).astype(jnp.int32) + (sec < sections - 1).astype(jnp.int32)
    )
    pl.semaphore_wait(barrier, greetings)

    def share_rims(m):
        @pl.when(has_above)
        def _():
            fe_up(m).start()

        @pl.when(has_below)
        def _():
            fe_down(m).start()

    def reduce_and_share(m, _):
        reduce_in(m, 0)
        share_rims(m)
        return 0

    share_rims(0)
    w_copy(1).wait()
    w_copy(2).wait()
    for n in range(model // bottle):
        lanes = pl.ds(n * bottle, bottle)
        t1[:, lanes] = w1_ref[lanes, :].astype(F32).T.astype(BF)
        t3[lanes, :] = w3_ref[:, lanes].astype(F32).T.astype(BF)
    for n in range(9):
        band = pl.ds(n * bottle, bottle)
        t2[band, :] = w2_ref[band, :].astype(F32).T.astype(BF)
    clear_rim(g_pad)

    def take_edges(m):
        @pl.when(has_above)
        def _():
            fe_down(m).wait_recv()
            act_pad[m, 0, pl.ds(PAD, cols)] = fe_in[m, 0].astype(F32)

        @pl.when(has_below)
        def _():
            fe_up(m).wait_recv()
            act_pad[m, rows + 1, pl.ds(PAD, cols)] = fe_in[m, 1].astype(F32)

    def expand_part(m, begin, width):
        span = pl.ds(begin, width)
        area = rows * width
        for shift in range(3):
            for y in range(rows + 2):
                taps[shift, m, y, span] = act_pad[m, y, pl.ds(PAD - 1 + shift + begin, width)].astype(BF)
        patch = jnp.concatenate(
            [
                taps[dx, m, pl.ds(dy, rows), span].reshape(area, bottle)
                for dy in range(3)
                for dx in range(3)
            ],
            axis=-1,
        )
        pre = dot_nn(patch, w2_ref[...]) + b2_ref[...]
        act, slope = silu_and_slope(pre)
        slope2[m, :, span] = slope.reshape(rows, width, bottle)
        act = act.astype(BF)
        act2[m, :, span] = act.reshape(rows, width, bottle)
        for n in range(model // bottle):
            lanes = pl.ds(n * bottle, bottle)
            pre = dot_nn(act, w3_ref[:, lanes]) + b3_ref[:, lanes]
            pre = pre + x_ref[m, :, span, lanes].reshape(area, bottle).astype(F32)
            slope3[m, :, span, lanes] = silu_and_slope(pre)[1].reshape(rows, width, bottle)

    def expand_out(m, _):
        take_edges(m)
        expand_part(m, 0, cols)
        return 0

    def outer_part(m, first, last):
        begin = cuts[first][0]
        width = sum(cuts[last]) - begin
        span = pl.ds(begin, width)
        for y in range(rows):
            g3[m, y, span] = (up[m, y, span].astype(F32) * slope3[m, y, span]).astype(BF)
        back = dot_nn(g3[m, :, span].reshape(rows * width, model), t3[...])
        grad = (back.reshape(rows, width, bottle) * slope2[m, :, span]).astype(BF)
        g2[m, :, span] = grad
        g_pad[m, pl.ds(1, rows), pl.ds(PAD + begin, width)] = grad.astype(F32)
        be_out[m, 0, span] = grad[0]
        be_out[m, 1, span] = grad[rows - 1]

    def send_rims(m, first, last):
        @pl.when(has_above)
        def _():
            for j in range(first, last + 1):
                be_up(m, j).start()

        @pl.when(has_below)
        def _():
            for j in range(first, last + 1):
                be_down(m, j).start()

    def take_rims(m, j):
        @pl.when(has_above)
        def _():
            be_down(m, j).wait_recv()
            g_pad[m, 0, pl.ds(PAD + cuts[j][0], cuts[j][1])] = be_in[m, 0, cut(j)].astype(F32)

        @pl.when(has_below)
        def _():
            be_up(m, j).wait_recv()
            g_pad[m, rows + 1, pl.ds(PAD + cuts[j][0], cuts[j][1])] = be_in[m, 1, cut(j)].astype(F32)

    def inner_part(m, first, last):
        begin = cuts[first][0]
        width = sum(cuts[last]) - begin
        span = pl.ds(begin, width)
        moved = [
            g_pad[m, :, pl.ds(PAD + 1 + begin - dx, width)].astype(BF) for dx in range(3)
        ]
        patch = jnp.concatenate(
            [
                moved[dx][2 - dy : 2 - dy + rows].reshape(rows * width, bottle)
                for dy in range(3)
                for dx in range(3)
            ],
            axis=-1,
        )
        total = dot_nn(patch, t2[...])
        grad = (total.reshape(rows, width, bottle) * slope1[m, :, span]).astype(BF)
        g1[m, :, span] = grad
        flat = grad.reshape(rows * width, bottle)
        for n in range(model // bottle):
            lanes = pl.ds(n * bottle, bottle)
            back = dot_nn(flat, t1[:, lanes]).reshape(rows, width, bottle)
            direct = up[m, :, span, lanes].astype(F32) * slope3[m, :, span, lanes]
            gin_ref[m, :, span, lanes] = (back + direct).astype(BF)

    def send_grads(m, first, last):
        @pl.when(sec > 0)
        def _():
            for j in range(first, last + 1):
                relay(m, j).start()

        if last == pieces - 1:
            gin_copy(m).start()

    def add_up(total, where, left, right, first, last):
        deep = (last - first) * pixels
        value = dot_tn(left.reshape(deep, bottle), right.reshape(deep, bottle))
        if first > 0:
            value = value + total[where]
        total[where] = value

    def add_three(n, first, last):
        lanes = pl.ds(n * bottle, bottle)
        ms = pl.ds(first, last - first)
        add_up(sum3, (slice(None), lanes), act2[ms], g3[ms, :, :, lanes], first, last)

    def add_two(n, first, last):
        ms = pl.ds(first, last - first)
        patch = taps[n % 3, ms, pl.ds(n // 3, rows)]
        add_up(sum2, (pl.ds(n * bottle, bottle), slice(None)), patch, g2[ms], first, last)

    def add_one(n, first, last):
        lanes = pl.ds(n * bottle, bottle)
        ms = pl.ds(first, last - first)
        add_up(sum1, (lanes, slice(None)), x_ref[ms, :, :, lanes], g1[ms], first, last)

    count = model // bottle
    threes = [functools.partial(add_three, n) for n in range(count)]
    twos = [functools.partial(add_two, n) for n in range(9)]
    ones = [functools.partial(add_one, n) for n in range(count)]
    adds = threes + twos + ones
    final = micros - 1

    kinds = (
        (sum3, p3, q3, r3, u3, d3, o3_ref),
        (sum2, p2, q2, r2, u2, d2, o2_ref),
        (sum1, p1, q1, r1, u1, d1, o1_ref),
    )

    def swap(kind):
        return remote(kinds[kind][1], kinds[kind][2], a_ss.at[kind], a_rs.at[kind], {"tile": partner})

    def hop_down(kind, d):
        n = kind * half + d
        return remote(
            kinds[kind][3].at[d], kinds[kind][4].at[d], z_ss.at[n], zd_rs.at[n], {"tile": tile + 2}
        )

    def hop_up(kind, d):
        n = kind * half + d
        return remote(
            kinds[kind][3].at[d], kinds[kind][5].at[d], z_ss.at[n], zu_rs.at[n], {"tile": tile - 2}
        )

    def start_swap(kind):
        total, sent, out = kinds[kind][0], kinds[kind][1], kinds[kind][6]
        span = out.shape[0]
        for z in range(half):
            first = pl.multiple_of((2 * z + 1 - core) * span, 16)
            sent[z] = total[pl.ds(first, span)].astype(BF)
        swap(kind).start()

    def make_part(kind):
        total, _, got, part, _, _, out = kinds[kind]
        span = out.shape[0]
        swap(kind).wait_recv()
        for z in range(half):
            first = pl.multiple_of((2 * z + core) * span, 16)
            part[z] = (total[pl.ds(first, span)] + got[z].astype(F32)).astype(BF)
        own = pl.multiple_of((2 * zed + core) * span, 16)
        out[...] = total[pl.ds(own, span)] + got[zed].astype(F32)

    def send_ends(kind, step):
        @pl.when(jnp.logical_not(chip_above))
        def _():
            hop_down(kind, half - 1 - step).start()

        @pl.when(jnp.logical_not(chip_below))
        def _():
            hop_up(kind, step).start()

    def carry_down(kind, step):
        part, down = kinds[kind][3], kinds[kind][4]
        d = half - 1 - step

        @pl.when(jnp.logical_and(chip_above, zed < d))
        def _():
            hop_down(kind, d).wait_recv()
            part[d] = (part[d].astype(F32) + down[d].astype(F32)).astype(BF)
            hop_down(kind, d).start()

    def carry_up(kind, step):
        part, over = kinds[kind][3], kinds[kind][5]

        @pl.when(jnp.logical_and(chip_below, zed > step))
        def _():
            hop_up(kind, step).wait_recv()
            part[step] = (part[step].astype(F32) + over[step].astype(F32)).astype(BF)
            hop_up(kind, step).start()

    def end_chain(kind):
        _, _, _, _, down, over, out = kinds[kind]

        @pl.when(chip_above)
        def _():
            hop_down(kind, zed).wait_recv()
            out[...] += down[zed].astype(F32)

        @pl.when(chip_below)
        def _():
            hop_up(kind, zed).wait_recv()
            out[...] += over[zed].astype(F32)

    def lead(first):
        for add in twos:
            add(first, micros)
        start_swap(1)
        for add in threes:
            add(first, micros)
        start_swap(0)

    def trail(first):
        for add in ones:
            add(first, micros)
        start_swap(2)

    @pl.when(is_last)
    def _():
        def stream(m, _):
            take_edges(m)
            cot_copy(m).wait()
            early = min(GROUP, pieces - 1)
            for first, last in ((0, early), (early + 1, pieces - 1)):
                if first <= last:
                    begin = cuts[first][0]
                    expand_part(m, begin, sum(cuts[last]) - begin)
                    outer_part(m, first, last)
                    send_rims(m, first, last)
            taken = 0
            for first in range(0, pieces, GROUP):
                last = min(first + GROUP, pieces) - 1
                until = min(last + 2, pieces)
                for j in range(taken, until):
                    take_rims(m, j)
                taken = until
                inner_part(m, first, last)
                send_grads(m, first, last)

            @pl.when(m == 0)
            def _():
                lax.fori_loop(1, micros, reduce_and_share, 0)

            return 0

        lax.fori_loop(0, micros, stream, 0)

    @pl.when(jnp.logical_not(is_last))
    def _():
        lax.fori_loop(1, micros, reduce_and_share, 0)
        lax.fori_loop(0, micros, expand_out, 0)

        def stream(m, _):
            left = list(adds)
            for j in range(pieces):
                relay(m, j).wait_recv()
                k = j - LAG - 1
                if j >= LAG:
                    take_rims(m, j - LAG)
                if k >= 0:
                    outer_part(m, j, j)
                    inner_part(m, k, k)
                    send_rims(m, j, j)
                    send_grads(m, k, k)
                else:
                    @pl.when(m == 0)
                    def _():
                        outer_part(m, j, j)

                    @pl.when(m > 0)
                    def _():
                        if j < LAG:
                            take_rims(m - 1, pieces + j - LAG)
                        outer_part(m, j, j)
                        inner_part(m - 1, pieces + k, pieces + k)

                    send_rims(m, j, j)

                    @pl.when(m > 0)
                    def _():
                        send_grads(m - 1, pieces + k, pieces + k)

                if k >= 0 and left:
                    share = -(-len(left) // (pieces - j))

                    @pl.when(jnp.logical_and(m == final, sec == 0))
                    def _():
                        for add in left[:share]:
                            add(0, final)

                    left = left[share:]
            return 0

        lax.fori_loop(0, micros, stream, 0)

    alone = jnp.logical_and(sec == 0, jnp.logical_not(is_last))

    @pl.when(alone)
    def _():
        lead(final)

    @pl.when(alone)
    def _():
        for j in range(pieces - LAG, pieces):
            take_rims(final, j)
        inner_part(final, pieces - LAG - 1, pieces - 1)
        send_grads(final, pieces - LAG - 1, pieces - 1)
        trail(final)

    @pl.when(jnp.logical_and(sec > 0, jnp.logical_not(is_last)))
    def _():
        for j in range(pieces - LAG, pieces):
            take_rims(final, j)
            last = j if j == pieces - 1 else j - 1
            inner_part(final, j - 1, last)
            send_grads(final, j - 1, last)

    @pl.when(jnp.logical_not(alone))
    def _():
        lead(0)
        trail(0)

    make_part(1)
    send_ends(1, 0)
    make_part(0)
    send_ends(0, 0)

    make_part(2)
    send_ends(2, 0)
    order = (1, 0, 2)
    for step in range(1, half - 1):
        for kind in order:
            send_ends(kind, step)
    upper = zed < half // 2
    for near, carries in ((upper, (carry_down, carry_up)), (jnp.logical_not(upper), (carry_up, carry_down))):
        @pl.when(near)
        def _():
            for step in range(half - 1):
                for carry in carries:
                    for kind in order:
                        carry(kind, step)


    def close(m, _):
        gin_copy(m).wait()

        @pl.when(has_above)
        def _():
            fe_up(m).wait_send()
            for j in range(pieces):
                be_up(m, j).wait_send()

        @pl.when(has_below)
        def _():
            fe_down(m).wait_send()
            for j in range(pieces):
                be_down(m, j).wait_send()

        @pl.when(sec > 0)
        def _():
            for j in range(pieces):
                relay(m, j).wait_send()

        return 0

    lax.fori_loop(0, micros, close, 0)
    for kind in range(3):
        end_chain(kind)
    for kind in range(3):
        swap(kind).wait_send()
        for d in range(half):
            @pl.when(zed < d)
            def _():
                hop_down(kind, d).wait_send()

            @pl.when(zed > d)
            def _():
                hop_up(kind, d).wait_send()


def cut_columns(cols):
    return [(n, WIDTH) for n in range(0, cols, WIDTH)]


def hand_over(*refs):
    count = len(refs) // 3
    ins, outs, sems = (refs[n * count : (n + 1) * count] for n in range(3))
    copies = [pltpu.make_async_copy(a, o, s) for a, o, s in zip(ins, outs, sems)]
    for copy in copies:
        copy.start()
    for copy in copies:
        copy.wait()


def local(
    sections, tiles,
    stored_inputs, cotangent, w_reduce, w_spatial, w_expand, bias_reduce, bias_spatial, bias_expand,
):
    _, micros, rows, cols, model = stored_inputs.shape
    bottle = w_reduce.shape[2]
    half = tiles // 2
    spans = (model // tiles, 9 * bottle // tiles, bottle // tiles)
    wides = (bottle, bottle, model)
    vmem = pltpu.VMEM
    dma = pltpu.SemaphoreType.DMA
    whole = pl.BlockSpec(memory_space=pltpu.VMEM)
    there = pl.BlockSpec(memory_space=pl.ANY)
    scratch = [
        vmem((micros, rows, cols, model), BF),
        vmem((model, bottle), BF),
        vmem((9 * bottle, bottle), BF),
        vmem((bottle, model), BF),
        vmem((micros, rows, cols, model), BF),
        vmem((micros, rows, cols, model), BF),
        vmem((micros, rows, cols, bottle), F32),
        vmem((micros, rows, cols, bottle), F32),
        vmem((micros, rows, cols, model), F32),
        vmem((micros, rows + 2, cols + 2 * PAD, bottle), F32),
        vmem((3, micros, rows + 2, cols, bottle), BF),
        vmem((micros, rows, cols, bottle), BF),
        vmem((micros, rows + 2, cols + 2 * PAD, bottle), F32),
        vmem((micros, rows, cols, model), BF),
        vmem((micros, rows, cols, bottle), BF),
        vmem((micros, rows, cols, bottle), BF),
    ]
    scratch += [vmem((bottle, model), BF), vmem((9 * bottle, bottle), BF), vmem((model, bottle), BF)]
    scratch += [vmem((micros, 2, cols, bottle), BF)] * 4
    scratch += [vmem((span * tiles, wide), F32) for span, wide in zip(spans, wides)]
    for _ in range(5):
        scratch += [vmem((half, span, wide), BF) for span, wide in zip(spans, wides)]
    pieces = micros * len(cut_columns(cols))
    scratch += [
        dma((micros,)), dma((3,)), dma((micros,)),
        dma((micros,)), dma((pieces,)), dma((pieces,)), dma((micros, 2)), dma((micros, 2)),
        dma((pieces, 2)), dma((pieces, 2)), dma((3,)), dma((3,)), dma((3 * half,)), dma((3 * half,)), dma((3 * half,)),
    ]
    shapes = [jax.ShapeDtypeStruct((micros, rows, cols, model), BF)] + [
        jax.ShapeDtypeStruct((span, wide), F32) for span, wide in zip(spans, wides)
    ]
    outs = pl.pallas_call(
        functools.partial(kernel, sections, tiles),
        out_shape=[vmem(shape.shape, shape.dtype) for shape in shapes],
        in_specs=[there] * 5 + [whole] * 3,
        out_specs=[there] + [whole] * 3,
        scratch_shapes=scratch,
        compiler_params=pltpu.CompilerParams(
            collective_id=0, has_side_effects=True, vmem_limit_bytes=58 * 1024 * 1024
        ),
    )(
        stored_inputs[0], cotangent, w_reduce[0], w_spatial[0], w_expand[0],
        bias_reduce, bias_spatial, bias_expand,
    )
    outs = pl.pallas_call(
        hand_over,
        out_shape=shapes,
        in_specs=[there] * 4,
        out_specs=[there] * 4,
        scratch_shapes=[dma] * 4,
        compiler_params=pltpu.CompilerParams(vmem_limit_bytes=2 * 1024 * 1024),
    )(*[pltpu.with_memory_space_constraint(out, pltpu.VMEM) for out in outs])
    return tuple(out[None] for out in outs)


def solution(mesh):
    return jax.shard_map(
        functools.partial(local, mesh.shape["section"], mesh.shape["tile"]),
        mesh=mesh,
        in_specs=(
            P("section", None, "tile", None, None),
            P(None, "tile", None, None),
            P("section", None, None),
            P("section", None, None),
            P("section", None, None),
            P("section", None),
            P("section", None),
            P("section", None),
        ),
        out_specs=(
            P("section", None, "tile", None, None),
            P("section", "tile", None),
            P("section", "tile", None),
            P("section", "tile", None),
        ),
        check_vma=False,
    )
```

```python
import functools

import jax
import jax.numpy as jnp
from jax import lax
from jax.experimental import pallas as pl
from jax.experimental.pallas import tpu as pltpu
from jax.sharding import PartitionSpec as P

BF = jnp.bfloat16
F32 = jnp.float32
PAD = 8
WIDTH = 8
LAG = 3
GROUP = 2


def silu_and_slope(pre_act):
    sigma_val = jax.nn.sigmoid(pre_act)
    return pre_act * sigma_val, sigma_val * (1.0 + pre_act * (1.0 - sigma_val))


def dot_nn(left, right):
    return jnp.dot(left, right, preferred_element_type=F32)


def dot_tn(left, right):
    return lax.dot_general(left, right, (((0,), (0,)), ((), ())), preferred_element_type=F32)


def kernel(
    sections, tiles, x_in, cot_ref, w1_in, w2_in, w3_in, b1_ref, b2_ref, b3_ref,
    gin_out, o1_ref, o2_ref, o3_ref,
    x_ref, w1_ref, w2_ref, w3_ref, gin_ref,
    up, slope1, slope2, slope3, act_pad, taps, act2, g_pad, g3, g2, g1,
    t1, t2, t3, fe_out, fe_in, be_out, be_in, sum1, sum2, sum3,
    p1, p2, p3, q1, q2, q3, r1, r2, r3, u1, u2, u3, d1, d2, d3,
    x_sem, w_sem, gin_sem, cot_sem, up_ss, up_rs, fe_ss, fe_rs, be_ss, be_rs, a_ss, a_rs, z_ss, zu_rs, zd_rs,
):
    micros, rows, cols, model = x_ref.shape
    bottle = w1_ref.shape[1]
    pixels = rows * cols
    cuts = cut_columns(cols)
    pieces = len(cuts)
    half = tiles // 2
    sec = lax.axis_index("section")
    tile = lax.axis_index("tile")
    core = lax.rem(tile, 2)
    zed = tile // 2
    is_last = sec == sections - 1
    has_above = tile > 0
    has_below = tile < tiles - 1
    chip_above = zed > 0
    chip_below = zed < half - 1
    partner = tile + 1 - 2 * core

    def x_copy(m):
        return pltpu.make_async_copy(x_in.at[m], x_ref.at[m], x_sem.at[m])

    def w_copy(n):
        src, dst = ((w1_in, w1_ref), (w2_in, w2_ref), (w3_in, w3_ref))[n]
        return pltpu.make_async_copy(src, dst, w_sem.at[n])

    def cot_copy(m):
        return pltpu.make_async_copy(cot_ref.at[m], up.at[m], cot_sem.at[m])

    def gin_copy(m):
        return pltpu.make_async_copy(gin_ref.at[m], gin_out.at[m], gin_sem.at[m])

    w_copy(0).start()
    x_copy(0).start()
    barrier = pltpu.get_barrier_semaphore()

    def greet(cond, target):
        @pl.when(cond)
        def _():
            pl.semaphore_signal(barrier, inc=1, device_id=target, device_id_type=pl.DeviceIdType.MESH)

    greet(has_above, {"tile": tile - 1})
    greet(has_below, {"tile": tile + 1})
    greet(chip_above, {"tile": tile - 2})
    greet(chip_below, {"tile": tile + 2})
    greet(sec > 0, {"section": sec - 1})
    greet(sec < sections - 1, {"section": sec + 1})

    def clear_rim(pad):
        tall, wide = pad.shape[1], pad.shape[2]
        for m in range(micros):
            for y in (0, tall - 1):
                pad[m, y] = jnp.zeros((wide, bottle), F32)
            for y in range(1, tall - 1):
                for c in (0, wide - PAD):
                    pad[m, y, pl.ds(c, PAD)] = jnp.zeros((PAD, bottle), F32)

    clear_rim(act_pad)

    def remote(src, dst, ss, rs, target):
        return pltpu.make_async_remote_copy(
            src_ref=src, dst_ref=dst, send_sem=ss, recv_sem=rs,
            device_id=target, device_id_type=pl.DeviceIdType.MESH,
        )

    def fe_up(m):
        return remote(fe_out.at[m, 0], fe_in.at[m, 1], fe_ss.at[m, 0], fe_rs.at[m, 1], {"tile": tile - 1})

    def fe_down(m):
        return remote(fe_out.at[m, 1], fe_in.at[m, 0], fe_ss.at[m, 1], fe_rs.at[m, 0], {"tile": tile + 1})

    def cut(j):
        return pl.ds(*cuts[j])

    def be_up(m, j):
        n = m * pieces + j
        return remote(
            be_out.at[m, 0, cut(j)], be_in.at[m, 1, cut(j)], be_ss.at[n, 0], be_rs.at[n, 1],
            {"tile": tile - 1},
        )

    def be_down(m, j):
        n = m * pieces + j
        return remote(
            be_out.at[m, 1, cut(j)], be_in.at[m, 0, cut(j)], be_ss.at[n, 1], be_rs.at[n, 0],
            {"tile": tile + 1},
        )

    def relay(m, j):
        n = m * pieces + j
        return remote(
            gin_ref.at[m, :, cut(j)], up.at[m, :, cut(j)], up_ss.at[n], up_rs.at[n],
            {"section": sec - 1},
        )

    def reduce_in(m, _):
        pre = dot_nn(x_ref[m].reshape(pixels, model), w1_ref[...]) + b1_ref[...]
        act, slope = silu_and_slope(pre)
        slope1[m] = slope.reshape(rows, cols, bottle)
        act = act.astype(BF).reshape(rows, cols, bottle)
        act_pad[m, pl.ds(1, rows), pl.ds(PAD, cols)] = act.astype(F32)
        fe_out[m, 0] = act[0]
        fe_out[m, 1] = act[rows - 1]
        return 0

    w_copy(0).wait()
    x_copy(0).wait()
    w_copy(1).start()
    w_copy(2).start()
    for m in range(1, micros):
        x_copy(m).start()

    @pl.when(is_last)
    def _():
        for m in range(micros):
            cot_copy(m).start()

    reduce_in(0, 0)

    greetings = (
        has_above.astype(jnp.int32) + has_below.astype(jnp.int32) + chip_above.astype(jnp.int32)
        + chip_below.astype(jnp.int32) + (sec > 0).astype(jnp.int32) + (sec < sections - 1).astype(jnp.int32)
    )
    pl.semaphore_wait(barrier, greetings)

    def share_rims(m):
        @pl.when(has_above)
        def _():
            fe_up(m).start()

        @pl.when(has_below)
        def _():
            fe_down(m).start()

    def reduce_and_share(m, _):
        x_copy(m).wait()
        reduce_in(m, 0)
        share_rims(m)
        return 0

    share_rims(0)
    w_copy(1).wait()
    w_copy(2).wait()
    for n in range(model // bottle):
        lanes = pl.ds(n * bottle, bottle)
        t1[:, lanes] = w1_ref[lanes, :].astype(F32).T.astype(BF)
        t3[lanes, :] = w3_ref[:, lanes].astype(F32).T.astype(BF)
    for n in range(9):
        band = pl.ds(n * bottle, bottle)
        t2[band, :] = w2_ref[band, :].astype(F32).T.astype(BF)
    clear_rim(g_pad)

    def take_edges(m):
        @pl.when(has_above)
        def _():
            fe_down(m).wait_recv()
            act_pad[m, 0, pl.ds(PAD, cols)] = fe_in[m, 0].astype(F32)

        @pl.when(has_below)
        def _():
            fe_up(m).wait_recv()
            act_pad[m, rows + 1, pl.ds(PAD, cols)] = fe_in[m, 1].astype(F32)

    def expand_part(m, begin, width):
        span = pl.ds(begin, width)
        area = rows * width
        for shift in range(3):
            for y in range(rows + 2):
                taps[shift, m, y, span] = act_pad[m, y, pl.ds(PAD - 1 + shift + begin, width)].astype(BF)
        patch = jnp.concatenate(
            [
                taps[dx, m, pl.ds(dy, rows), span].reshape(area, bottle)
                for dy in range(3)
                for dx in range(3)
            ],
            axis=-1,
        )
        pre = dot_nn(patch, w2_ref[...]) + b2_ref[...]
        act, slope = silu_and_slope(pre)
        slope2[m, :, span] = slope.reshape(rows, width, bottle)
        act = act.astype(BF)
        act2[m, :, span] = act.reshape(rows, width, bottle)
        for n in range(model // bottle):
            lanes = pl.ds(n * bottle, bottle)
            pre = dot_nn(act, w3_ref[:, lanes]) + b3_ref[:, lanes]
            pre = pre + x_ref[m, :, span, lanes].reshape(area, bottle).astype(F32)
            slope3[m, :, span, lanes] = silu_and_slope(pre)[1].reshape(rows, width, bottle)

    def expand_out(m, _):
        take_edges(m)
        expand_part(m, 0, cols)
        return 0

    def outer_part(m, first, last):
        begin = cuts[first][0]
        width = sum(cuts[last]) - begin
        span = pl.ds(begin, width)
        for y in range(rows):
            g3[m, y, span] = (up[m, y, span].astype(F32) * slope3[m, y, span]).astype(BF)
        back = dot_nn(g3[m, :, span].reshape(rows * width, model), t3[...])
        grad = (back.reshape(rows, width, bottle) * slope2[m, :, span]).astype(BF)
        g2[m, :, span] = grad
        g_pad[m, pl.ds(1, rows), pl.ds(PAD + begin, width)] = grad.astype(F32)
        be_out[m, 0, span] = grad[0]
        be_out[m, 1, span] = grad[rows - 1]

    def send_rims(m, first, last):
        @pl.when(has_above)
        def _():
            for j in range(first, last + 1):
                be_up(m, j).start()

        @pl.when(has_below)
        def _():
            for j in range(first, last + 1):
                be_down(m, j).start()

    def take_rims(m, j):
        @pl.when(has_above)
        def _():
            be_down(m, j).wait_recv()
            g_pad[m, 0, pl.ds(PAD + cuts[j][0], cuts[j][1])] = be_in[m, 0, cut(j)].astype(F32)

        @pl.when(has_below)
        def _():
            be_up(m, j).wait_recv()
            g_pad[m, rows + 1, pl.ds(PAD + cuts[j][0], cuts[j][1])] = be_in[m, 1, cut(j)].astype(F32)

    def inner_part(m, first, last):
        begin = cuts[first][0]
        width = sum(cuts[last]) - begin
        span = pl.ds(begin, width)
        moved = [
            g_pad[m, :, pl.ds(PAD + 1 + begin - dx, width)].astype(BF) for dx in range(3)
        ]
        patch = jnp.concatenate(
            [
                moved[dx][2 - dy : 2 - dy + rows].reshape(rows * width, bottle)
                for dy in range(3)
                for dx in range(3)
            ],
            axis=-1,
        )
        total = dot_nn(patch, t2[...])
        grad = (total.reshape(rows, width, bottle) * slope1[m, :, span]).astype(BF)
        g1[m, :, span] = grad
        flat = grad.reshape(rows * width, bottle)
        for n in range(model // bottle):
            lanes = pl.ds(n * bottle, bottle)
            back = dot_nn(flat, t1[:, lanes]).reshape(rows, width, bottle)
            direct = up[m, :, span, lanes].astype(F32) * slope3[m, :, span, lanes]
            gin_ref[m, :, span, lanes] = (back + direct).astype(BF)

    def send_grads(m, first, last):
        @pl.when(sec > 0)
        def _():
            for j in range(first, last + 1):
                relay(m, j).start()

        if last == pieces - 1:
            gin_copy(m).start()

    def add_up(total, where, left, right, first, last):
        deep = (last - first) * pixels
        value = dot_tn(left.reshape(deep, bottle), right.reshape(deep, bottle))
        if first > 0:
            value = value + total[where]
        total[where] = value

    def add_three(n, first, last):
        lanes = pl.ds(n * bottle, bottle)
        ms = pl.ds(first, last - first)
        add_up(sum3, (slice(None), lanes), act2[ms], g3[ms, :, :, lanes], first, last)

    def add_two(n, first, last):
        ms = pl.ds(first, last - first)
        patch = taps[n % 3, ms, pl.ds(n // 3, rows)]
        add_up(sum2, (pl.ds(n * bottle, bottle), slice(None)), patch, g2[ms], first, last)

    def add_one(n, first, last):
        lanes = pl.ds(n * bottle, bottle)
        ms = pl.ds(first, last - first)
        add_up(sum1, (lanes, slice(None)), x_ref[ms, :, :, lanes], g1[ms], first, last)

    count = model // bottle
    threes = [functools.partial(add_three, n) for n in range(count)]
    twos = [functools.partial(add_two, n) for n in range(9)]
    ones = [functools.partial(add_one, n) for n in range(count)]
    adds = threes + twos + ones
    final = micros - 1

    kinds = (
        (sum3, p3, q3, r3, u3, d3, o3_ref),
        (sum2, p2, q2, r2, u2, d2, o2_ref),
        (sum1, p1, q1, r1, u1, d1, o1_ref),
    )

    def swap(kind):
        return remote(kinds[kind][1], kinds[kind][2], a_ss.at[kind], a_rs.at[kind], {"tile": partner})

    def hop_down(kind, d):
        n = kind * half + d
        return remote(
            kinds[kind][3].at[d], kinds[kind][4].at[d], z_ss.at[n], zd_rs.at[n], {"tile": tile + 2}
        )

    def hop_up(kind, d):
        n = kind * half + d
        return remote(
            kinds[kind][3].at[d], kinds[kind][5].at[d], z_ss.at[n], zu_rs.at[n], {"tile": tile - 2}
        )

    def start_swap(kind):
        total, sent, out = kinds[kind][0], kinds[kind][1], kinds[kind][6]
        span = out.shape[0]
        for z in range(half):
            first = pl.multiple_of((2 * z + 1 - core) * span, 16)
            sent[z] = total[pl.ds(first, span)].astype(BF)
        swap(kind).start()

    def make_part(kind):
        total, _, got, part, _, _, out = kinds[kind]
        span = out.shape[0]
        swap(kind).wait_recv()
        for z in range(half):
            first = pl.multiple_of((2 * z + core) * span, 16)
            part[z] = (total[pl.ds(first, span)] + got[z].astype(F32)).astype(BF)
        own = pl.multiple_of((2 * zed + core) * span, 16)
        out[...] = total[pl.ds(own, span)] + got[zed].astype(F32)

    def send_ends(kind, step):
        @pl.when(jnp.logical_not(chip_above))
        def _():
            hop_down(kind, half - 1 - step).start()

        @pl.when(jnp.logical_not(chip_below))
        def _():
            hop_up(kind, step).start()

    def carry_down(kind, step):
        part, down = kinds[kind][3], kinds[kind][4]
        d = half - 1 - step

        @pl.when(jnp.logical_and(chip_above, zed < d))
        def _():
            hop_down(kind, d).wait_recv()
            part[d] = (part[d].astype(F32) + down[d].astype(F32)).astype(BF)
            hop_down(kind, d).start()

    def carry_up(kind, step):
        part, over = kinds[kind][3], kinds[kind][5]

        @pl.when(jnp.logical_and(chip_below, zed > step))
        def _():
            hop_up(kind, step).wait_recv()
            part[step] = (part[step].astype(F32) + over[step].astype(F32)).astype(BF)
            hop_up(kind, step).start()

    def end_chain(kind):
        _, _, _, _, down, over, out = kinds[kind]

        @pl.when(chip_above)
        def _():
            hop_down(kind, zed).wait_recv()
            out[...] += down[zed].astype(F32)

        @pl.when(chip_below)
        def _():
            hop_up(kind, zed).wait_recv()
            out[...] += over[zed].astype(F32)

    def lead(first):
        for add in twos:
            add(first, micros)
        start_swap(1)
        for add in threes:
            add(first, micros)
        start_swap(0)

    def trail(first):
        for add in ones:
            add(first, micros)
        start_swap(2)

    @pl.when(is_last)
    def _():
        def stream(m, _):
            take_edges(m)
            cot_copy(m).wait()
            early = min(GROUP, pieces - 1)
            for first, last in ((0, early), (early + 1, pieces - 1)):
                if first <= last:
                    begin = cuts[first][0]
                    expand_part(m, begin, sum(cuts[last]) - begin)
                    outer_part(m, first, last)
                    send_rims(m, first, last)
            taken = 0
            for first in range(0, pieces, GROUP):
                last = min(first + GROUP, pieces) - 1
                until = min(last + 2, pieces)
                for j in range(taken, until):
                    take_rims(m, j)
                taken = until
                inner_part(m, first, last)
                send_grads(m, first, last)

            @pl.when(m == 0)
            def _():
                lax.fori_loop(1, micros, reduce_and_share, 0)

            return 0

        lax.fori_loop(0, micros, stream, 0)

    @pl.when(jnp.logical_not(is_last))
    def _():
        lax.fori_loop(1, micros, reduce_and_share, 0)
        lax.fori_loop(0, micros, expand_out, 0)

        def stream(m, _):
            left = list(adds)
            for j in range(pieces):
                relay(m, j).wait_recv()
                k = j - LAG - 1
                if j >= LAG:
                    take_rims(m, j - LAG)
                if k >= 0:
                    outer_part(m, j, j)
                    inner_part(m, k, k)
                    send_rims(m, j, j)
                    send_grads(m, k, k)
                else:
                    @pl.when(m == 0)
                    def _():
                        outer_part(m, j, j)

                    @pl.when(m > 0)
                    def _():
                        if j < LAG:
                            take_rims(m - 1, pieces + j - LAG)
                        outer_part(m, j, j)
                        inner_part(m - 1, pieces + k, pieces + k)

                    send_rims(m, j, j)

                    @pl.when(m > 0)
                    def _():
                        send_grads(m - 1, pieces + k, pieces + k)

                if k >= 0 and left:
                    share = -(-len(left) // max(1, pieces - GROUP - LAG - j))

                    @pl.when(jnp.logical_and(m == final, sec == 0))
                    def _():
                        for add in left[:share]:
                            add(0, final)

                    left = left[share:]
            return 0

        lax.fori_loop(0, micros, stream, 0)

    alone = jnp.logical_and(sec == 0, jnp.logical_not(is_last))

    @pl.when(alone)
    def _():
        lead(final)
        make_part(1)
        send_ends(1, 0)

    @pl.when(alone)
    def _():
        for j in range(pieces - LAG, pieces):
            take_rims(final, j)
        inner_part(final, pieces - LAG - 1, pieces - 1)
        send_grads(final, pieces - LAG - 1, pieces - 1)
        trail(final)

    @pl.when(jnp.logical_and(sec > 0, jnp.logical_not(is_last)))
    def _():
        for j in range(pieces - LAG, pieces):
            take_rims(final, j)
            last = j if j == pieces - 1 else j - 1
            inner_part(final, j - 1, last)
            send_grads(final, j - 1, last)

    @pl.when(jnp.logical_not(alone))
    def _():
        lead(0)
        make_part(1)
        send_ends(1, 0)
        trail(0)

    make_part(0)
    send_ends(0, 0)

    make_part(2)
    send_ends(2, 0)
    order = (1, 0, 2)
    for step in range(1, half - 1):
        for kind in order:
            send_ends(kind, step)
    upper = zed < half // 2
    for near, carries in ((upper, (carry_down, carry_up)), (jnp.logical_not(upper), (carry_up, carry_down))):
        @pl.when(near)
        def _():
            for step in range(half - 1):
                for carry in carries:
                    for kind in order:
                        carry(kind, step)


    def close(m, _):
        gin_copy(m).wait()

        @pl.when(has_above)
        def _():
            fe_up(m).wait_send()
            for j in range(pieces):
                be_up(m, j).wait_send()

        @pl.when(has_below)
        def _():
            fe_down(m).wait_send()
            for j in range(pieces):
                be_down(m, j).wait_send()

        @pl.when(sec > 0)
        def _():
            for j in range(pieces):
                relay(m, j).wait_send()

        return 0

    lax.fori_loop(0, micros, close, 0)
    for kind in range(3):
        end_chain(kind)
    for kind in range(3):
        swap(kind).wait_send()
        for d in range(half):
            @pl.when(zed < d)
            def _():
                hop_down(kind, d).wait_send()

            @pl.when(zed > d)
            def _():
                hop_up(kind, d).wait_send()


def cut_columns(cols):
    return [(n, WIDTH) for n in range(0, cols, WIDTH)]


def hand_over(*refs):
    count = len(refs) // 3
    ins, outs, sems = (refs[n * count : (n + 1) * count] for n in range(3))
    copies = [
        pltpu.make_async_copy(ins[0].at[m, y], outs[0].at[m, y], sems[0].at[m, y])
        for m in range(ins[0].shape[0])
        for y in range(ins[0].shape[1])
    ]
    copies += [pltpu.make_async_copy(a, o, s) for a, o, s in zip(ins[1:], outs[1:], sems[1:])]
    for copy in copies:
        copy.start()
    for copy in copies:
        copy.wait()


def local(
    sections, tiles,
    stored_inputs, cotangent, w_reduce, w_spatial, w_expand, bias_reduce, bias_spatial, bias_expand,
):
    _, micros, rows, cols, model = stored_inputs.shape
    bottle = w_reduce.shape[2]
    half = tiles // 2
    spans = (model // tiles, 9 * bottle // tiles, bottle // tiles)
    wides = (bottle, bottle, model)
    vmem = pltpu.VMEM
    dma = pltpu.SemaphoreType.DMA
    whole = pl.BlockSpec(memory_space=pltpu.VMEM)
    there = pl.BlockSpec(memory_space=pl.ANY)
    scratch = [
        vmem((micros, rows, cols, model), BF),
        vmem((model, bottle), BF),
        vmem((9 * bottle, bottle), BF),
        vmem((bottle, model), BF),
        vmem((micros, rows, cols, model), BF),
        vmem((micros, rows, cols, model), BF),
        vmem((micros, rows, cols, bottle), F32),
        vmem((micros, rows, cols, bottle), F32),
        vmem((micros, rows, cols, model), F32),
        vmem((micros, rows + 2, cols + 2 * PAD, bottle), F32),
        vmem((3, micros, rows + 2, cols, bottle), BF),
        vmem((micros, rows, cols, bottle), BF),
        vmem((micros, rows + 2, cols + 2 * PAD, bottle), F32),
        vmem((micros, rows, cols, model), BF),
        vmem((micros, rows, cols, bottle), BF),
        vmem((micros, rows, cols, bottle), BF),
    ]
    scratch += [vmem((bottle, model), BF), vmem((9 * bottle, bottle), BF), vmem((model, bottle), BF)]
    scratch += [vmem((micros, 2, cols, bottle), BF)] * 4
    scratch += [vmem((span * tiles, wide), F32) for span, wide in zip(spans, wides)]
    for _ in range(5):
        scratch += [vmem((half, span, wide), BF) for span, wide in zip(spans, wides)]
    pieces = micros * len(cut_columns(cols))
    scratch += [
        dma((micros,)), dma((3,)), dma((micros,)),
        dma((micros,)), dma((pieces,)), dma((pieces,)), dma((micros, 2)), dma((micros, 2)),
        dma((pieces, 2)), dma((pieces, 2)), dma((3,)), dma((3,)), dma((3 * half,)), dma((3 * half,)), dma((3 * half,)),
    ]
    shapes = [jax.ShapeDtypeStruct((micros, rows, cols, model), BF)] + [
        jax.ShapeDtypeStruct((span, wide), F32) for span, wide in zip(spans, wides)
    ]
    outs = pl.pallas_call(
        functools.partial(kernel, sections, tiles),
        out_shape=[vmem(shape.shape, shape.dtype) for shape in shapes],
        in_specs=[there] * 5 + [whole] * 3,
        out_specs=[there] + [whole] * 3,
        scratch_shapes=scratch,
        compiler_params=pltpu.CompilerParams(
            collective_id=0, has_side_effects=True, vmem_limit_bytes=58 * 1024 * 1024
        ),
    )(
        stored_inputs[0], cotangent, w_reduce[0], w_spatial[0], w_expand[0],
        bias_reduce, bias_spatial, bias_expand,
    )
    outs = pl.pallas_call(
        hand_over,
        out_shape=shapes,
        in_specs=[there] * 4,
        out_specs=[there] * 4,
        scratch_shapes=[dma((micros, rows))] + [dma] * 3,
        compiler_params=pltpu.CompilerParams(vmem_limit_bytes=2 * 1024 * 1024),
    )(*[pltpu.with_memory_space_constraint(out, pltpu.VMEM) for out in outs])
    return tuple(out[None] for out in outs)


def solution(mesh):
    return jax.shard_map(
        functools.partial(local, mesh.shape["section"], mesh.shape["tile"]),
        mesh=mesh,
        in_specs=(
            P("section", None, "tile", None, None),
            P(None, "tile", None, None),
            P("section", None, None),
            P("section", None, None),
            P("section", None, None),
            P("section", None),
            P("section", None),
            P("section", None),
        ),
        out_specs=(
            P("section", None, "tile", None, None),
            P("section", "tile", None),
            P("section", "tile", None),
            P("section", "tile", None),
        ),
        check_vma=False,
    )
```
